32 devices in a mesh: grp: 4 (over y, x), line: 8 (over z, core).
Axes of the slice: x: 2, y: 2, z: 4, core: 2. Of those that a mesh axis runs over, the one named last changes fastest.
Arguments:
- velocity: bfloat16 [3, 1536, 96, 512], P(None, 'line', 'grp'), may hold values from -6 to 6
- vorticity: bfloat16 [3, 1536, 96, 512], P(None, 'line', 'grp'), may hold values from -6 to 6
- wall_velocity: float32 [2, 256, 96, 1536], P(None, ('grp', 'line')), may hold values from -6 to 6
- wall_vorticity: float32 [2, 256, 96, 1536], P(None, ('grp', 'line')), may hold values from -6 to 6
- keep_mask: int32 [256, 96], P(('grp', 'line')), may hold values from 0 to 1, as said below
- derivative_band: float32 [7, 1536], replicated, may hold values from -3 to 3
- eigenvalues: float32 [1536], replicated, may hold values from 0.25 to 4
- eigenbasis: float32 [1536, 1536], replicated, may hold values from -0.15625 to 0.15625
Outputs:
- new_velocity: float32 [2, 256, 96, 1536], P(None, ('grp', 'line'))
- new_vorticity: float32 [2, 256, 96, 1536], P(None, ('grp', 'line'))
The draws below stay inside these ranges and needn't reach their ends.
Inputs may be any that keep to these rules, and one draw needn't show every extreme that they name: keep_mask is 0 wherever kx >= 170, or 32 <= kz < 64.
All inputs are finite; a program needn't handle non-finite values.
Results may differ from the reference program's by a relative error of at most 0.0003.
Values sent between devices are 32-bit elements; how exact they have to be, the bound alone decides.
A program may use at most 384 MiB of HBM per device.

```python
import math
import jax
import jax.numpy as jnp
from jax import lax

NY = 1536
PX = 512
PZ = 96
KX = 256


def draw_keep_mask(key, part):
    random_bits = jax.random.randint(key, (KX, PZ), 0, 4)
    stream_index = jnp.arange(KX, dtype=jnp.int32)[:, None]
    span_index = jnp.arange(PZ, dtype=jnp.int32)[None, :]
    inside = (stream_index < 2 * KX // 3) & ((span_index < PZ // 3) | (span_index >= PZ - PZ // 3))
    return jnp.where(inside & (random_bits > 0), 1, 0).astype(jnp.int32)


def block_levels(rng, extent, cuts, low, high):
    def one(axis_at, blocks):
        heights = jax.random.uniform(jax.random.fold_in(jax.random.fold_in(rng, 6), axis_at), (blocks,), jnp.float32, low / len(cuts), high / len(cuts))
        return jnp.repeat(jnp.exp(heights), extent[axis_at] // blocks).reshape((-1,) + (1,) * (len(extent) - axis_at - 1))

    gain = one(*cuts[0])
    for cut in cuts[1:]:
        gain = gain * one(*cut)
    return gain


def centred(stream_key, dims, width, most, split=(), held_as=jnp.bfloat16):
    result = width * jax.random.normal(stream_key, dims, jnp.float32)
    if split:
        result = result * block_levels(stream_key, dims, split, -0.22, 0.18)
    return jnp.clip(result, -most, most).astype(held_as)


def setup_inputs(seed: int = 0) -> dict:
    arg_keys = jax.random.split(jax.random.key(seed), 9)
    velocity = centred(arg_keys[0], (3, NY, PZ, PX), 1.0, 6.0, ((1, 8), (2, 4)))
    vorticity = centred(arg_keys[1], (3, NY, PZ, PX), 1.0, 6.0, ((1, 8), (2, 4)))
    wall_velocity = centred(arg_keys[2], (2, KX, PZ, NY), 1.0, 6.0, ((1, 32),), jnp.float32)
    wall_vorticity = centred(arg_keys[3], (2, KX, PZ, NY), 1.0, 6.0, ((1, 32),), jnp.float32)
    keep_mask = draw_keep_mask(jax.random.fold_in(arg_keys[8], 71), 0)
    derivative_band = centred(arg_keys[5], (7, NY), 0.5, 3.0, (), jnp.float32)
    eigenvalues = jnp.clip(jnp.exp(jax.random.uniform(arg_keys[6], (NY,), jnp.float32, math.log(0.25), math.log(4.0))), 0.25, 4.0)
    eigenbasis = centred(arg_keys[7], (NY, NY), NY ** -0.5, 0.15625, (), jnp.float32)
    return dict(velocity=velocity, vorticity=vorticity, wall_velocity=wall_velocity, wall_vorticity=wall_vorticity, keep_mask=keep_mask, derivative_band=derivative_band, eigenvalues=eigenvalues, eigenbasis=eigenbasis)


HIGHEST_PRECISION = lax.Precision.HIGHEST

def phase_table(number, points):
    index_rows = jnp.arange(number, dtype=jnp.int32)[:, None]
    index_cols = jnp.arange(points, dtype=jnp.int32)[None, :]
    phase_angle = (index_rows * index_cols % points).astype(jnp.float32) * (2.0 * math.pi / points)
    norm_scale = 1.0 / math.sqrt(points)
    return (jnp.cos(phase_angle) * norm_scale, jnp.sin(phase_angle) * norm_scale)

def reference(velocity, vorticity, wall_velocity, wall_vorticity, keep_mask, derivative_band, eigenvalues, eigenbasis):
    stream_cosine, stream_sine = phase_table(KX, PX)
    span_cosine, span_sine = phase_table(PZ, PZ)
    slab_depth = math.gcd(NY, 16)
    blocks = NY // slab_depth

    def slab_modes(pieces):
        moving = pieces[0].astype(jnp.float32)
        turning = pieces[1].astype(jnp.float32)
        lamb_vector = jnp.stack([moving[1] * turning[2] - moving[2] * turning[1], moving[2] * turning[0] - moving[0] * turning[2], moving[0] * turning[1] - moving[1] * turning[0]])
        real_part = jnp.einsum('fyzx,kx->fyzk', lamb_vector, stream_cosine, precision=HIGHEST_PRECISION)
        imag_part = -jnp.einsum('fyzx,kx->fyzk', lamb_vector, stream_sine, precision=HIGHEST_PRECISION)
        out_real = jnp.einsum('qz,fyzk->fkqy', span_cosine, real_part, precision=HIGHEST_PRECISION) + jnp.einsum('qz,fyzk->fkqy', span_sine, imag_part, precision=HIGHEST_PRECISION)
        out_imag = jnp.einsum('qz,fyzk->fkqy', span_cosine, imag_part, precision=HIGHEST_PRECISION) - jnp.einsum('qz,fyzk->fkqy', span_sine, real_part, precision=HIGHEST_PRECISION)
        return jnp.stack([out_real, out_imag], 1)
    moving_blocks = velocity.reshape(3, blocks, slab_depth, PZ, PX).transpose(1, 0, 2, 3, 4)
    turning_blocks = vorticity.reshape(3, blocks, slab_depth, PZ, PX).transpose(1, 0, 2, 3, 4)
    mapped = lax.map(slab_modes, (moving_blocks, turning_blocks))
    modes = mapped.transpose(1, 2, 3, 4, 0, 5).reshape(3, 2, KX, PZ, NY)
    stream_wave = (jnp.arange(KX, dtype=jnp.int32).astype(jnp.float32) / KX)[:, None, None]
    span_index = jnp.arange(PZ, dtype=jnp.int32)
    span_wave = (jnp.where(span_index < PZ // 2, span_index, span_index - PZ).astype(jnp.float32) / (PZ / 2.0))[:, None]
    wave_square = stream_wave * stream_wave + span_wave * span_wave
    slope_source = jnp.stack([-stream_wave * modes[0, 1] - span_wave * modes[2, 1], stream_wave * modes[0, 0] + span_wave * modes[2, 0]])
    normal_term = jnp.stack([-span_wave * modes[0, 1] + stream_wave * modes[2, 1], span_wave * modes[0, 0] - stream_wave * modes[2, 0]])
    padded = jnp.pad(slope_source, ((0, 0), (0, 0), (0, 0), (3, 3)))
    wall_slope = derivative_band[0] * padded[..., 0:NY]
    for offset in range(1, 7):
        wall_slope = wall_slope + derivative_band[offset] * padded[..., offset:offset + NY]
    keep_weight = keep_mask.astype(jnp.float32)[:, :, None]
    right_velocity = wall_velocity + keep_weight * (wave_square * modes[1] - wall_slope)
    right_vorticity = wall_vorticity + keep_weight * normal_term

    def helmholtz(right_side):
        eigen_coeffs = jnp.einsum('pkqy,yj->pkqj', right_side, eigenbasis, precision=HIGHEST_PRECISION)
        eigen_coeffs = eigen_coeffs / (eigenvalues + wave_square)
        return jnp.einsum('pkqj,yj->pkqy', eigen_coeffs, eigenbasis, precision=HIGHEST_PRECISION)
    return (helmholtz(right_velocity), helmholtz(right_vorticity))
```

```python
import math

import jax
import jax.numpy as jnp
from jax import lax
from jax.experimental import pallas as pl
from jax.experimental.pallas import tpu as pltpu
from jax.sharding import PartitionSpec as P


CHUNKS = 6
AHEAD = 3
REACH = 3
HIGH = lax.Precision.HIGH


def phase_table(indices, points, places=None):
    if places is None:
        places = jnp.arange(points, dtype=jnp.int32)
    index_cols = places[None, :]
    phase_angle = (indices[:, None] * index_cols % points).astype(jnp.float32) * (
        2.0 * math.pi / points
    )
    norm_scale = 1.0 / math.sqrt(points)
    return (jnp.cos(phase_angle) * norm_scale, jnp.sin(phase_angle) * norm_scale)


def signed_wave(indices, points):
    signed_index = jnp.where(indices < points // 2, indices, indices - points)
    return signed_index.astype(jnp.float32) / (points / 2.0)


def split_table(table):
    high = lax.reduce_precision(table, 8, 7)
    return high.astype(jnp.bfloat16), (table - high).astype(jnp.bfloat16)


def split_value(value):
    high = value.astype(jnp.bfloat16)
    return high, (value - high.astype(jnp.float32)).astype(jnp.bfloat16)


def mul(left, right):
    return lax.dot_general(
        left, right, (((1,), (0,)), ((), ())), preferred_element_type=jnp.float32
    )


def stream_kernel(u_ref, w_ref, high_ref, low_ref, *out_refs):
    rows, span, width = out_refs[0].shape[1:]
    u = [u_ref[f].astype(jnp.float32) for f in range(3)]
    w = [w_ref[f].astype(jnp.float32) for f in range(3)]
    high, low = high_ref[...], low_ref[...]
    for f in range(3):
        a, b = (f + 1) % 3, (f + 2) % 3
        lamb = u[a] * w[b] - u[b] * w[a]
        lamb = lamb.reshape(rows * span, lamb.shape[-1])
        lamb_high, lamb_low = split_value(lamb)
        spectra = mul(lamb_high, low) + mul(lamb_low, high) + mul(lamb_high, high)
        for g, out_ref in enumerate(out_refs):
            out_ref[f] = spectra[:, g * width : (g + 1) * width].reshape(rows, span, width)


def stream_stage(velocity, vorticity, table, groups, width, chunk):
    _, depth, span, points = velocity.shape
    rows_all = depth // CHUNKS
    rows = math.gcd(rows_all, 8)
    steps = rows_all // rows
    source = pl.BlockSpec((3, rows, span, points), lambda i: (0, chunk * steps + i, 0, 0))
    whole = pl.BlockSpec(table[0].shape, lambda i: (0, 0))
    return pl.pallas_call(
        stream_kernel,
        grid=(steps,),
        in_specs=[source, source, whole, whole],
        out_specs=[pl.BlockSpec((3, rows, span, width), lambda i: (0, i, 0, 0))] * groups,
        out_shape=[jax.ShapeDtypeStruct((3, rows_all, span, width), jnp.float32)] * groups,
        cost_estimate=pl.CostEstimate(
            flops=18 * rows_all * span * points * table[0].shape[1],
            bytes_accessed=12 * rows_all * span * (points + groups * width),
            transcendentals=0,
        ),
        compiler_params=pltpu.CompilerParams(vmem_limit_bytes=48 * 1024 * 1024),
        name="stream",
    )(velocity, vorticity, *table)


def make_span_kernel(steps, rows, lines, line_modes):
    def kernel(
        band_ref, wide_ref, low_ref, ax_ref, az_ref, sign_ref, slope_in, rest_in, *refs
    ):
        plane_refs = refs[:-5]
        out_ref, slope_out, rest_out, slope_ref, rest_ref = refs[-5:]
        step = pl.program_id(0)
        kept, width = ax_ref.shape

        @pl.when(step == 0)
        def _():
            slope_ref[0 : 2 * REACH] = slope_in[...]
            rest_ref[0:REACH] = rest_in[...]

        @pl.when(step > 0)
        def _():
            for r in range(2 * REACH):
                slope_ref[r] = slope_ref[rows + r]
            for r in range(REACH):
                rest_ref[r] = rest_ref[rows + r]

        @pl.when(step < steps)
        def _():
            ax, az, sign = ax_ref[...], az_ref[...], sign_ref[...]
            square = ax * ax + az * az

            for r in range(rows):
                plane = jnp.concatenate(
                    [
                        jnp.concatenate([plane_ref[f, r] for plane_ref in plane_refs], 0)
                        for f in range(3)
                    ],
                    1,
                )
                high, low = split_value(plane)
                both = mul(wide_ref[...], jnp.concatenate([high, low], 0)) + mul(
                    low_ref[...], high
                )
                cosine = [both[:kept, f * width : (f + 1) * width] for f in range(3)]
                sine = [both[kept:, f * width : (f + 1) * width] for f in range(3)]
                half = width // 2
                slope_ref[2 * REACH + r] = (ax * sine[0] + az * sine[2]) - sign * pltpu.roll(
                    ax * cosine[0] + az * cosine[2], half, 1
                )
                rest_ref[REACH + r, 0] = square * (cosine[1] + sign * pltpu.roll(sine[1], half, 1))
                rest_ref[REACH + r, 1] = (az * sine[0] - ax * sine[2]) - sign * pltpu.roll(
                    az * cosine[0] - ax * cosine[2], half, 1
                )

        @pl.when(step >= steps)
        def _():
            for r in range(rows):
                slope_ref[2 * REACH + r] = jnp.zeros((kept, width), jnp.float32)
                rest_ref[REACH + r] = jnp.zeros((2, kept, width), jnp.float32)

        group_modes = width // 2
        for r in range(rows):
            total = rest_ref[r, 0]
            for d in range(2 * REACH + 1):
                total = total - band_ref[d, step * rows + r] * slope_ref[r + d]
            turned = jnp.concatenate([total, rest_ref[r, 1]], 0).T
            for p in range(2):
                for line in range(lines):
                    at = p * group_modes + line * line_modes
                    out_ref[line, r, p] = turned[at : at + line_modes]

        slope_out[...] = slope_ref[rows : rows + 2 * REACH]
        rest_out[...] = rest_ref[rows : rows + REACH]

    return kernel


def span_stage(planes, band, wide, low, ax, az, sign, carry, lines, flush):
    sources = len(planes)
    _, rows_all, span, width = planes[0].shape
    kept = ax.shape[0]
    rows = math.gcd(rows_all, 8)
    steps = rows_all // rows
    extra = -(-2 * REACH // rows) if flush else 0
    line_modes = width // 2 // lines
    whole = lambda shape: pl.BlockSpec(shape, lambda i: (0,) * len(shape))
    held = [
        jax.ShapeDtypeStruct((2 * REACH, kept, width), jnp.float32),
        jax.ShapeDtypeStruct((REACH, 2, kept, width), jnp.float32),
    ]
    rows_out = (steps + extra) * rows
    return pl.pallas_call(
        make_span_kernel(steps, rows, lines, line_modes),
        grid=(steps + extra,),
        in_specs=[
            pl.BlockSpec(memory_space=pltpu.SMEM),
            whole(wide.shape),
            whole(low.shape),
            whole(ax.shape),
            whole(az.shape),
            whole(sign.shape),
            whole(held[0].shape),
            whole(held[1].shape),
        ]
        + [
            pl.BlockSpec(
                (3, rows, span, width), lambda i: (0, jnp.minimum(i, steps - 1), 0, 0)
            )
        ]
        * sources,
        out_specs=[
            pl.BlockSpec((lines, rows, 2, line_modes, 2 * kept), lambda i: (0, i, 0, 0, 0)),
            whole(held[0].shape),
            whole(held[1].shape),
        ],
        out_shape=[
            jax.ShapeDtypeStruct((lines, rows_out, 2, line_modes, 2 * kept), jnp.float32)
        ]
        + held,
        scratch_shapes=[
            pltpu.VMEM((rows + 2 * REACH, kept, width), jnp.float32),
            pltpu.VMEM((rows + REACH, 2, kept, width), jnp.float32),
        ],
        cost_estimate=pl.CostEstimate(
            flops=40 * rows_all * sources * span * width * kept,
            bytes_accessed=12 * rows_all * span * sources * width,
            transcendentals=0,
        ),
        compiler_params=pltpu.CompilerParams(vmem_limit_bytes=48 * 1024 * 1024),
        name="spanwise",
    )(band, wide, low, ax, az, sign, *carry, *planes)


def local(
    velocity,
    vorticity,
    wall_velocity,
    wall_vorticity,
    keep_mask,
    derivative_band,
    eigenvalues,
    eigenbasis,
):
    groups = lax.axis_size("grp")
    lines = lax.axis_size("line")
    group_index = lax.axis_index("grp")
    line_index = lax.axis_index("line")
    depth, span_share, stream_points = velocity.shape[1:]
    span_points = span_share * groups
    stream_modes = stream_points // 2
    group_modes = stream_modes // groups
    line_modes = group_modes // lines
    wall_points = wall_velocity.shape[3]
    width = 2 * group_modes
    span_keep = span_points // 3
    kept = 2 * span_keep
    live_groups = min(groups, -(-(2 * stream_modes // 3) // group_modes))

    partners = group_index ^ jnp.arange(groups, dtype=jnp.int32)
    partner_modes = (
        partners[:, None] * group_modes + jnp.arange(group_modes, dtype=jnp.int32)
    ).reshape(-1)
    cosine, sine = phase_table(partner_modes, stream_points)
    stream_table = jnp.stack(
        [
            cosine.reshape(groups, group_modes, stream_points),
            -sine.reshape(groups, group_modes, stream_points),
        ],
        1,
    ).reshape(2 * stream_modes, stream_points)
    stream_table = split_table(stream_table.T)

    span_list = jnp.concatenate(
        [
            jnp.arange(span_keep, dtype=jnp.int32),
            jnp.arange(span_points - span_keep, span_points, dtype=jnp.int32),
        ]
    )
    places = (
        partners[:, None] * span_share + jnp.arange(span_share, dtype=jnp.int32)
    ).reshape(-1)
    span_high, span_low = split_table(
        jnp.concatenate(phase_table(span_list, span_points, places), 0)
    )
    span_wide = jnp.concatenate([span_high, span_high], 1)
    mode_at = group_index * group_modes + jnp.arange(group_modes, dtype=jnp.int32)
    ax = mode_at.astype(jnp.float32) / stream_modes
    ax = jnp.broadcast_to(jnp.concatenate([ax, ax])[None, :], (kept, width))
    az = jnp.broadcast_to(signed_wave(span_list, span_points)[:, None], (kept, width))
    sign = jnp.where(jnp.arange(width) < group_modes, 1.0, -1.0).astype(jnp.float32)
    sign = jnp.broadcast_to(sign[None, :], (kept, width))

    pad_rows = 2 * REACH + 8
    band_padded = jnp.pad(derivative_band, ((0, 0), (pad_rows, pad_rows)))
    basis_padded = jnp.pad(eigenbasis, ((pad_rows, pad_rows), (0, 0)))

    chunk_rows = depth // CHUNKS
    carry = (
        jnp.zeros((2 * REACH, kept, width), jnp.float32),
        jnp.zeros((REACH, 2, kept, width), jnp.float32),
    )
    spectra = [
        stream_stage(velocity, vorticity, stream_table, groups, width, chunk)
        for chunk in range(CHUNKS)
    ]
    planes = []
    for own in spectra:
        blocks = [own[0]]
        for d in range(1, groups):
            pairs = [(g, g ^ d) for g in range(groups) if g ^ d < live_groups]
            blocks.append(lax.ppermute(own[d], "grp", pairs))
        planes.append(blocks)
    walls = [wall_velocity, wall_vorticity]
    wall_coeffs = []
    arrived = None
    for chunk in range(CHUNKS):
        flush = chunk == CHUNKS - 1
        rows = math.gcd(chunk_rows, 8)
        rows_out = chunk_rows + (-(-2 * REACH // rows) * rows if flush else 0)
        start = pad_rows + line_index * depth + chunk * chunk_rows - REACH
        band = lax.dynamic_slice_in_dim(band_padded, start, rows_out, 1)
        if chunk == 0:
            ahead = [planes[c][0] for c in range(1, min(AHEAD, CHUNKS - 1) + 1)]
            *ahead, band = lax.optimization_barrier((*ahead, band))
            for c, block in enumerate(ahead, 1):
                planes[c][0] = block
        elif chunk + AHEAD < CHUNKS:
            planes[chunk + AHEAD][0], band = lax.optimization_barrier(
                (planes[chunk + AHEAD][0], band)
            )
        if chunk < len(walls):
            coeffs = jnp.einsum("pkqy,yj->pkqj", walls[chunk], eigenbasis, precision=HIGH)
            coeffs, band = lax.optimization_barrier((coeffs, band))
            wall_coeffs.append(coeffs)
        out, *carry = span_stage(
            planes[chunk], band, span_wide, span_low, ax, az, sign, carry, lines, flush
        )
        whole_lines = lax.all_to_all(out, "line", split_axis=0, concat_axis=0, tiled=True)
        first = pad_rows + chunk * chunk_rows - REACH
        basis = jnp.stack(
            [
                lax.slice_in_dim(basis_padded, first + s * depth, first + s * depth + rows_out)
                for s in range(lines)
            ]
        ).reshape(lines * rows_out, wall_points)
        part = jnp.einsum(
            "yr,yj->rj",
            whole_lines.reshape(lines * rows_out, -1),
            basis,
            precision=HIGH,
        )
        arrived = part if arrived is None else arrived + part
    arrived = arrived.reshape(2, line_modes, 2, kept, wall_points)

    device_modes = (group_index * lines + line_index) * line_modes + jnp.arange(
        line_modes, dtype=jnp.int32
    )
    device_wave = (device_modes.astype(jnp.float32) / stream_modes)[:, None, None]
    full_wave = signed_wave(jnp.arange(span_points, dtype=jnp.int32), span_points)[:, None]
    full_square = device_wave * device_wave + full_wave * full_wave
    keep_weight = keep_mask.astype(jnp.float32)[:, :, None]
    solved = []
    for field, coeffs in enumerate(wall_coeffs):
        forced = arrived[:, :, field]
        middle = jnp.zeros(
            (2, line_modes, span_points - kept, wall_points), jnp.float32
        )
        forced = jnp.concatenate([forced[:, :, :span_keep], middle, forced[:, :, span_keep:]], 2)
        coeffs = (coeffs + keep_weight * forced) / (eigenvalues + full_square)
        solved.append(jnp.einsum("pkqj,yj->pkqy", coeffs, eigenbasis, precision=HIGH))
    return tuple(solved)


def solution(mesh):
    placed = (
        P(None, "line", "grp", None),
        P(None, "line", "grp", None),
        P(None, ("grp", "line"), None, None),
        P(None, ("grp", "line"), None, None),
        P(("grp", "line"), None),
        P(),
        P(),
        P(),
    )

    return jax.shard_map(
        local,
        mesh=mesh,
        in_specs=placed,
        out_specs=(P(None, ("grp", "line"), None, None), P(None, ("grp", "line"), None, None)),
        check_vma=False,
    )
```
